32 devices in a mesh: days: 2 (over x), blk: 16 (over z, y, core).
Axes of the slice: x: 2, y: 2, z: 4, core: 2. Of those that a mesh axis runs over, the one named last changes fastest.
Arguments:
- traces: bfloat16 [2048, 8, 1024], P(('days', 'blk')), parts along dimension 0, may hold values from -6 to 6
- valid: int32 [32, 8], P(('days', 'blk')), parts along dimension 0, may hold values from 0 to 1, as said below
Outputs:
- correlations: bfloat16 [2, 32, 64, 64, 512], P(None, ('days', 'blk')), parts along dimension 1
The draws below stay inside these ranges and needn't reach their ends.
There are 2 independent parts, one for each index of `days`. The reference program is written for one: setup_inputs(seed, part) draws one part's arguments, and reference() takes and returns one part's arrays. A program takes and returns all parts, laid end to end along the dimension named above; each array names one. Nothing has to cross between parts.
Inputs may be any that keep to these rules, and one draw needn't show every extreme that they name: `valid`: in every draw one block, which one is drawn from the seed, has no usable window at all.
All inputs are finite; a program needn't handle non-finite values.
Results may differ from the reference program's by a relative error of at most 0.0089.
Values may be sent and summed in bfloat16 or wider, within the bound.
A program may use at most 128 MiB of HBM per device.

```python
import math
import jax
import jax.numpy as jnp
from jax import lax

CH = 64
WINDOW_SAMPLES = 1024
LAGS = 512
BAND = 64
ROUNDS = 2
TIME_WINDOWS = 8
FREQS = 512
BLOCKS = 16
CHANNELS = 1024


def draw_valid(key, part):
    mask_key = jax.random.fold_in(key, 11)
    pick_key = jax.random.fold_in(key, 23)
    levels = jax.random.randint(mask_key, (BLOCKS, TIME_WINDOWS), 0, 4, dtype=jnp.int32)
    usable = jnp.where(levels < 3, 1, 0).astype(jnp.int32)
    silent = jax.random.randint(pick_key, (), 0, BLOCKS, dtype=jnp.int32)
    rows = jnp.arange(BLOCKS, dtype=jnp.int32)[:, None]
    return jnp.where(rows == silent, 0, usable).astype(jnp.int32)


def shard_levels(key, extent, pieces, low, largest):
    level, own = 1.0, jax.random.fold_in(key, 6)
    for position, parts in pieces:
        draws = jnp.exp(jax.random.uniform(jax.random.fold_in(own, position), (parts,), jnp.float32, low / len(pieces), largest / len(pieces)))
        level = level * jnp.repeat(draws, extent[position] // parts).reshape([-1 if axis == position else 1 for axis in range(len(extent))])
    return level


def noise(own_key, dims, spread, bound, split=(), kind=jnp.bfloat16):
    entries = spread * jax.random.normal(own_key, dims, jnp.float32)
    if split:
        entries = entries * shard_levels(own_key, dims, split, -0.22, 0.18)
    return jnp.clip(entries, -bound, bound).astype(kind)


def setup_inputs(seed: int = 0, part: int = 0) -> dict:
    key_of = jax.random.split(jax.random.key(seed), 3)
    part_splits = jax.random.split(jax.random.fold_in(key_of[2], part), 3)
    traces = noise(part_splits[0], (CHANNELS, TIME_WINDOWS, WINDOW_SAMPLES), 1.0, 6.0, ((0, 16),))
    valid = draw_valid(jax.random.fold_in(jax.random.fold_in(key_of[2], part), 71), part)
    return {"traces": traces, "valid": valid}


epsilon = 1e-05

def forward_twiddles():
    samples = jnp.arange(WINDOW_SAMPLES, dtype=jnp.int32)
    bins = jnp.arange(FREQS, dtype=jnp.int32)
    phase = (samples[:, None] * bins[None, :] % WINDOW_SAMPLES).astype(jnp.float32) * (2.0 * math.pi / WINDOW_SAMPLES)
    table = jnp.concatenate([jnp.cos(phase), -jnp.sin(phase)], axis=1) / math.sqrt(WINDOW_SAMPLES)
    return table.astype(jnp.bfloat16)

def inverse_table():
    bins = jnp.arange(FREQS, dtype=jnp.int32)
    shifts = jnp.arange(LAGS, dtype=jnp.int32) - LAGS // 2
    phase = (bins[:, None] * shifts[None, :] % WINDOW_SAMPLES).astype(jnp.float32) * (2.0 * math.pi / WINDOW_SAMPLES)
    weight = jnp.where(bins == 0, 1.0, 2.0).astype(jnp.float32)[:, None] / math.sqrt(FREQS)
    table = jnp.concatenate([weight * jnp.cos(phase), -weight * jnp.sin(phase)], axis=0)
    return table.astype(jnp.bfloat16)

def whiten(traces, prior_sample, flags):
    pair_count = traces.shape[0]
    differenced_traces = (traces.astype(jnp.float32) - prior_sample.astype(jnp.float32)).astype(jnp.bfloat16)
    window_spectra = jnp.dot(differenced_traces.reshape(pair_count * TIME_WINDOWS, WINDOW_SAMPLES), forward_twiddles(), preferred_element_type=jnp.float32)
    window_spectra = window_spectra.reshape(pair_count, TIME_WINDOWS, 2 * FREQS)
    power = window_spectra[:, :, :FREQS] ** 2 + window_spectra[:, :, FREQS:] ** 2
    banded = lax.optimization_barrier(jnp.mean(power.reshape(pair_count, TIME_WINDOWS, FREQS // BAND, BAND), axis=-1))
    factor = jnp.repeat(lax.rsqrt(banded + epsilon), BAND, axis=-1) * flags[:, :, None]
    return (window_spectra * jnp.concatenate([factor, factor], axis=-1)).astype(jnp.bfloat16)

def correlate(own, partner, own_flags, partner_flags, inverse):
    highest = lax.Precision.HIGHEST
    own_real = own[:, :, :FREQS].astype(jnp.float32)
    own_imag = own[:, :, FREQS:].astype(jnp.float32)
    far_real = partner[:, :, :FREQS].astype(jnp.float32)
    far_imag = partner[:, :, FREQS:].astype(jnp.float32)
    real_part = jnp.einsum('iwf,jwf->fij', own_real, far_real, precision=highest) + jnp.einsum('iwf,jwf->fij', own_imag, far_imag, precision=highest)
    imag_part = jnp.einsum('iwf,jwf->fij', own_real, far_imag, precision=highest) - jnp.einsum('iwf,jwf->fij', own_imag, far_real, precision=highest)
    total = jnp.maximum(jnp.sum(own_flags * partner_flags), 1.0)
    stacked = (jnp.concatenate([real_part, imag_part], axis=0).reshape(2 * FREQS, CH * CH) / total).astype(jnp.bfloat16)
    result = lax.dot_general(stacked, inverse, (((0,), (0,)), ((), ())), preferred_element_type=jnp.float32)
    return result.reshape(CH, CH, LAGS).astype(jnp.bfloat16)

def reference(traces, valid):
    flags = valid.astype(jnp.float32)
    channel_flags = jnp.repeat(flags, CH, axis=0)
    prior_sample = jnp.concatenate([jnp.zeros((1, TIME_WINDOWS, WINDOW_SAMPLES), jnp.bfloat16), traces[:-1]], axis=0)
    whitened = whiten(traces, prior_sample, channel_flags).reshape(BLOCKS, CH, TIME_WINDOWS, 2 * FREQS)
    inverse = inverse_table()
    results = []
    for round_index in range(1, ROUNDS + 1):
        partner = jnp.roll(whitened, -round_index, axis=0)
        partner_flags = jnp.roll(flags, -round_index, axis=0)
        results.append(lax.map(lambda items: correlate(items[0], items[1], items[2], items[3], inverse), (whitened, partner, flags, partner_flags)))
    return jnp.stack(results, axis=0)
```

```python
import functools
import math

import jax
import jax.numpy as jnp
import numpy as np
from jax import lax
from jax.experimental import pallas as pl
from jax.experimental.pallas import tpu as pltpu
from jax.sharding import PartitionSpec as P

LAGS = 512
BAND = 64
ROUNDS = 2
epsilon = 1e-05
GROUP = 8
ROWS = 8


def forward_table(samples):
    bins = samples // 2
    phase = (np.arange(bins)[:, None] * np.arange(samples)[None, :] % samples) * (
        2.0 * math.pi / samples
    )
    cos = (np.cos(phase) / math.sqrt(samples)).reshape(bins // BAND, 1, BAND, samples)
    sin = (-np.sin(phase) / math.sqrt(samples)).reshape(bins // BAND, 1, BAND, samples)
    table = np.concatenate([cos, sin], axis=1).reshape(2 * bins, samples)
    return jnp.asarray(table.astype(np.float32), dtype=jnp.bfloat16)


def inverse_table(samples):
    bins = samples // 2
    shifts = np.arange(LAGS) - LAGS // 2
    phase = (np.arange(bins)[:, None] * shifts[None, :] % samples) * (2.0 * math.pi / samples)
    weight = np.where(np.arange(bins) == 0, 1.0, 2.0)[:, None] / math.sqrt(bins)
    table = np.concatenate([weight * np.cos(phase), -weight * np.sin(phase)], axis=0)
    return jnp.asarray(table.astype(np.float32), dtype=jnp.bfloat16)


def whiten_block(x, prior, flags, table_ref, diff_ref, rows_ref, y_ref):
    ch, windows, samples = x.shape
    bins = samples // 2
    wide = x.astype(jnp.float32)
    before = jnp.concatenate([prior.astype(jnp.float32), wide[:-1]], axis=0)
    diff = (wide - before).reshape(ch * windows, samples)
    lanes = diff_ref.shape[2]
    for q in range(samples // lanes):
        diff_ref[q] = diff[:, q * lanes : (q + 1) * lanes]
        for w in range(windows):
            rows_ref[w * ch : (w + 1) * ch, q * lanes : (q + 1) * lanes] = diff_ref[
                q, pl.ds(w, ch, stride=windows), :
            ].astype(jnp.bfloat16)
    bands = 2
    height = bands * 2 * BAND
    depth = 2 * windows

    @pl.loop(0, 2 * bins // height)
    def _(step):
        at = pl.multiple_of(step * height, height)
        product = lax.dot_general(
            table_ref[pl.ds(at, height), :],
            rows_ref[...],
            (((1,), (1,)), ((), ())),
            preferred_element_type=jnp.float32,
        )
        for k in range(bands):
            real = product[k * 2 * BAND : k * 2 * BAND + BAND]
            imag = product[k * 2 * BAND + BAND : (k + 1) * 2 * BAND]
            level = jnp.sum(real * real + imag * imag, axis=0, keepdims=True) * (1.0 / BAND)
            factor = lax.rsqrt(level + epsilon) * flags
            real = real * factor
            imag = imag * factor
            first = pl.multiple_of((step * bands + k) * BAND * depth, BAND * depth)
            for w in range(windows):
                re = real[:, w * ch : (w + 1) * ch]
                im = imag[:, w * ch : (w + 1) * ch]
                y_ref[pl.ds(first + w, BAND, stride=depth), :] = jnp.concatenate([re, im], axis=1)
                y_ref[pl.ds(first + windows + w, BAND, stride=depth), :] = jnp.concatenate(
                    [im, -re], axis=1
                )


def gather_kernel(
    n,
    x_ref,
    flag_ref,
    table_ref,
    own_ref,
    far_ref,
    scale_ref,
    own_x,
    far_x,
    last_x,
    far_flag,
    diff_ref,
    rows_ref,
    y_ref,
    copy_sem,
    send_sem,
    recv_sem,
):
    me = lax.axis_index("blk")
    ch, windows, samples = own_x.shape
    barrier = pltpu.get_barrier_semaphore()
    for step in (1, 2):
        for peer in (lax.rem(me + step, n), lax.rem(me + n - step, n)):
            pl.semaphore_signal(
                barrier, inc=1, device_id={"blk": peer}, device_id_type=pl.DeviceIdType.MESH
            )
    local = pltpu.make_async_copy(x_ref, own_x, copy_sem)
    local.start()
    pl.semaphore_wait(barrier, 4)

    def remote(src, dst, slot, peer):
        return pltpu.make_async_remote_copy(
            src_ref=src,
            dst_ref=dst,
            send_sem=send_sem.at[slot],
            recv_sem=recv_sem.at[slot],
            device_id={"blk": peer},
            device_id_type=pl.DeviceIdType.MESH,
        )

    last = remote(x_ref.at[pl.ds(ch - 1, 1)], last_x, 0, lax.rem(me + 1, n))
    last.start()
    sends = []
    for r in (1, 2):
        peer = lax.rem(me + n - r, n)
        flag = remote(flag_ref, far_flag.at[r - 1], 2 * r, peer)
        flag.start()
        body = remote(x_ref, far_x.at[r - 1], 2 * r - 1, peer)
        body.start()
        sends.append((flag, body))

    flags = flag_ref[0:1, :]
    zero_row = jnp.zeros((1, windows, samples), jnp.float32)
    local.wait()
    last.wait()
    prior = jnp.where(me == 0, zero_row, last_x[...].astype(jnp.float32))
    whiten_block(own_x[...], prior, flags, table_ref, diff_ref, rows_ref, y_ref)

    wide = GROUP * 2 * windows

    @pl.loop(0, own_ref.shape[0])
    def _(g):
        at = pl.multiple_of(g * wide, wide)
        own_ref[g] = y_ref[pl.ds(at, wide), :].T[:ch].astype(jnp.bfloat16)

    for r in (1, 2):
        flag, body = sends[r - 1]
        flag.wait()
        body.wait()
        other = far_flag[r - 1][0:1, :]
        ref = own_x if r == 1 else far_x.at[r - 2]
        row = ref[ch - 1 : ch].astype(jnp.float32)
        prior = jnp.where(lax.rem(me + r, n) == 0, zero_row, row)
        whiten_block(far_x[r - 1], prior, other, table_ref, diff_ref, rows_ref, y_ref)
        far_ref[r - 1] = y_ref[...].astype(jnp.bfloat16)
        count = jnp.sum(flags * other, axis=1, keepdims=True) * (1.0 / ch)
        scale_ref[r - 1] = jnp.broadcast_to(1.0 / jnp.maximum(count, 1.0), scale_ref.shape[1:])


def cross_kernel(own_ref, far_ref, scale_ref, inverse_ref, out_ref, t_ref):
    groups, ch, wide = own_ref.shape
    depth = wide // GROUP
    bins = groups * GROUP
    stage = pl.program_id(1)

    @pl.when(stage == 0)
    def _():
        scale = scale_ref[0][0:1, :]
        scale2 = jnp.concatenate([scale, scale], axis=1)

        @pl.loop(0, groups)
        def _(g):
            lhs = own_ref[g]
            far = far_ref[0, pl.ds(pl.multiple_of(g * wide, wide), wide), :]
            zero = jnp.zeros((depth, 2 * ch), jnp.bfloat16)
            for q in range(GROUP // 2):
                columns = []
                for h in (2 * q, 2 * q + 1):
                    parts = [zero] * GROUP
                    parts[h] = far[h * depth : (h + 1) * depth]
                    columns.append(jnp.concatenate(parts, axis=0))
                rhs = jnp.concatenate(columns, axis=1)
                cross = jnp.dot(lhs, rhs, preferred_element_type=jnp.float32) * scale2
                for s in (0, 1):
                    at = pl.multiple_of((g * GROUP + 2 * q + s) * ch, ch)
                    t_ref[pl.ds(at, ch), :] = cross[:, s * 2 * ch : (s + 1) * 2 * ch]

    @pl.when(stage > 0)
    def _():
        rows = out_ref.shape[1]
        per = 4

        @pl.loop(0, rows // per)
        def _(p):
            stacked = []
            for k in range(per):
                i = (stage - 1) * rows + p * per + k
                block = t_ref[pl.ds(i, bins, stride=ch), :].astype(jnp.bfloat16).T
                stacked.append(jnp.concatenate([block[:ch], block[ch:]], axis=1))
            lhs = jnp.concatenate(stacked, axis=0)
            result = jnp.dot(lhs, inverse_ref[...], preferred_element_type=jnp.float32)
            result = result.astype(jnp.bfloat16).reshape(per, ch, result.shape[1])
            out_ref[0, pl.ds(p * per, per)] = result


def shards(traces, valid):
    n = lax.axis_size("blk")
    ch, windows, samples = traces.shape
    bins = samples // 2
    depth = 2 * windows
    vmem = pl.BlockSpec(memory_space=pltpu.VMEM)
    flags = jnp.broadcast_to(
        jnp.repeat(valid.astype(jnp.float32), ch, axis=1), (8, ch * windows)
    )
    own, far, scale = pl.pallas_call(
        functools.partial(gather_kernel, n),
        out_shape=(
            jax.ShapeDtypeStruct((bins // GROUP, ch, GROUP * depth), jnp.bfloat16),
            jax.ShapeDtypeStruct((ROUNDS, bins * depth, 2 * ch), jnp.bfloat16),
            jax.ShapeDtypeStruct((ROUNDS, 8, 2 * ch), jnp.float32),
        ),
        in_specs=[pl.BlockSpec(memory_space=pl.ANY), vmem, vmem],
        out_specs=(vmem, vmem, vmem),
        scratch_shapes=[
            pltpu.VMEM((ch, windows, samples), jnp.bfloat16),
            pltpu.VMEM((ROUNDS, ch, windows, samples), jnp.bfloat16),
            pltpu.VMEM((1, windows, samples), jnp.bfloat16),
            pltpu.VMEM((ROUNDS, 8, ch * windows), jnp.float32),
            pltpu.VMEM((samples // 128, ch * windows, 128), jnp.float32),
            pltpu.VMEM((ch * windows, samples), jnp.bfloat16),
            pltpu.VMEM((bins * depth, 2 * ch), jnp.float32),
            pltpu.SemaphoreType.DMA,
            pltpu.SemaphoreType.DMA((5,)),
            pltpu.SemaphoreType.DMA((5,)),
        ],
        compiler_params=pltpu.CompilerParams(
            collective_id=0, has_side_effects=True, vmem_limit_bytes=48 << 20
        ),
        name="gather_whiten",
    )(traces, flags, forward_table(samples))
    stages = 1 + ch // ROWS
    result = pl.pallas_call(
        cross_kernel,
        grid=(ROUNDS, stages),
        out_shape=jax.ShapeDtypeStruct((ROUNDS, ch, ch, LAGS), jnp.bfloat16),
        in_specs=[
            pl.BlockSpec(own.shape, lambda r, s: (0, 0, 0)),
            pl.BlockSpec((1,) + far.shape[1:], lambda r, s: (r, 0, 0)),
            pl.BlockSpec((1,) + scale.shape[1:], lambda r, s: (r, 0, 0)),
            pl.BlockSpec((2 * bins, LAGS), lambda r, s: (0, 0)),
        ],
        out_specs=pl.BlockSpec(
            (1, ROWS, ch, LAGS), lambda r, s: (r, jnp.maximum(s - 1, 0), 0, 0)
        ),
        scratch_shapes=[pltpu.VMEM((bins * ch, 2 * ch), jnp.float32)],
        compiler_params=pltpu.CompilerParams(
            dimension_semantics=("arbitrary", "arbitrary"), vmem_limit_bytes=48 << 20
        ),
        name="cross_inverse",
    )(own, far, scale, inverse_table(samples))
    return result[:, None]


def solution(mesh):
    return jax.shard_map(
        shards,
        mesh=mesh,
        in_specs=(P(("days", "blk"), None, None), P(("days", "blk"), None)),
        out_specs=P(None, ("days", "blk"), None, None, None),
        check_vma=False,
    )
```

```python
import functools
import math

import jax
import jax.numpy as jnp
import numpy as np
from jax import lax
from jax.experimental import pallas as pl
from jax.experimental.pallas import tpu as pltpu
from jax.sharding import PartitionSpec as P

LAGS = 512
BAND = 64
ROUNDS = 2
epsilon = 1e-05
GROUP = 8
ROWS = 8
UNROLL = 4


def forward_table(samples):
    bins = samples // 2
    phase = (np.arange(bins)[:, None] * np.arange(samples)[None, :] % samples) * (
        2.0 * math.pi / samples
    )
    cos = (np.cos(phase) / math.sqrt(samples)).reshape(bins // BAND, 1, BAND, samples)
    sin = (-np.sin(phase) / math.sqrt(samples)).reshape(bins // BAND, 1, BAND, samples)
    table = np.concatenate([cos, sin], axis=1).reshape(2 * bins, samples)
    return jnp.asarray(table.astype(np.float32), dtype=jnp.bfloat16)


def inverse_table(samples):
    bins = samples // 2
    shifts = np.arange(LAGS) - LAGS // 2
    phase = (np.arange(bins)[:, None] * shifts[None, :] % samples) * (2.0 * math.pi / samples)
    weight = np.where(np.arange(bins) == 0, 1.0, 2.0)[:, None] / math.sqrt(bins)
    table = np.concatenate([weight * np.cos(phase), -weight * np.sin(phase)], axis=0)
    return jnp.asarray(table.astype(np.float32), dtype=jnp.bfloat16)


def whiten_block(x, prior, flags, table_ref, diff_ref, rows_ref, y_ref):
    ch, windows, samples = x.shape
    bins = samples // 2
    wide = x.astype(jnp.float32)
    before = jnp.concatenate([prior.astype(jnp.float32), wide[:-1]], axis=0)
    diff = wide - before
    lanes = diff_ref.shape[2]
    pitch = windows + 1
    for q in range(samples // lanes):
        for c in range(ch):
            diff_ref[q, c * pitch : c * pitch + windows] = diff[c, :, q * lanes : (q + 1) * lanes]
        for w in range(windows):
            rows_ref[w * ch : (w + 1) * ch, q * lanes : (q + 1) * lanes] = diff_ref[
                q, pl.ds(w, ch, stride=pitch), :
            ].astype(jnp.bfloat16)
    bands = 2
    height = bands * 2 * BAND
    pitch = 2 * windows + 1

    @pl.loop(0, 2 * bins // height)
    def _(step):
        at = pl.multiple_of(step * height, height)
        product = lax.dot_general(
            table_ref[pl.ds(at, height), :],
            rows_ref[...],
            (((1,), (1,)), ((), ())),
            preferred_element_type=jnp.float32,
        )
        for k in range(bands):
            real = product[k * 2 * BAND : k * 2 * BAND + BAND]
            imag = product[k * 2 * BAND + BAND : (k + 1) * 2 * BAND]
            level = jnp.sum(real * real + imag * imag, axis=0, keepdims=True) * (1.0 / BAND)
            factor = lax.rsqrt(level + epsilon) * flags
            real = real * factor
            imag = imag * factor
            first = pl.multiple_of((step * bands + k) * BAND * pitch, BAND * pitch)
            for w in range(windows):
                re = real[:, w * ch : (w + 1) * ch]
                im = imag[:, w * ch : (w + 1) * ch]
                y_ref[pl.ds(first + w, BAND, stride=pitch), :] = jnp.concatenate([re, im], axis=1)
                y_ref[pl.ds(first + windows + w, BAND, stride=pitch), :] = jnp.concatenate(
                    [im, -re], axis=1
                )


def gather_kernel(
    n,
    x_ref,
    flag_ref,
    table_ref,
    own_ref,
    far_ref,
    scale_ref,
    own_x,
    far_x,
    last_x,
    far_flag,
    diff_ref,
    rows_ref,
    y_ref,
    copy_sem,
    send_sem,
    recv_sem,
):
    me = lax.axis_index("blk")
    ch, windows, samples = own_x.shape
    barrier = pltpu.get_barrier_semaphore()
    for step in (1, 2):
        for peer in (lax.rem(me + step, n), lax.rem(me + n - step, n)):
            pl.semaphore_signal(
                barrier, inc=1, device_id={"blk": peer}, device_id_type=pl.DeviceIdType.MESH
            )
    local = pltpu.make_async_copy(x_ref, own_x, copy_sem)
    local.start()
    pl.semaphore_wait(barrier, 4)

    def remote(src, dst, slot, peer):
        return pltpu.make_async_remote_copy(
            src_ref=src,
            dst_ref=dst,
            send_sem=send_sem.at[slot],
            recv_sem=recv_sem.at[slot],
            device_id={"blk": peer},
            device_id_type=pl.DeviceIdType.MESH,
        )

    last = remote(x_ref.at[pl.ds(ch - 1, 1)], last_x, 0, lax.rem(me + 1, n))
    last.start()
    sends = []
    for r in (1, 2):
        peer = lax.rem(me + n - r, n)
        flag = remote(flag_ref, far_flag.at[r - 1], 2 * r, peer)
        flag.start()
        body = remote(x_ref, far_x.at[r - 1], 2 * r - 1, peer)
        body.start()
        sends.append((flag, body))

    flags = flag_ref[0:1, :]
    zero_row = jnp.zeros((1, windows, samples), jnp.float32)
    local.wait()
    last.wait()
    prior = jnp.where(me == 0, zero_row, last_x[...].astype(jnp.float32))
    whiten_block(own_x[...], prior, flags, table_ref, diff_ref, rows_ref, y_ref)

    groups = own_ref.shape[0]
    depth = 2 * windows
    wide = GROUP * depth

    def bins_of(g):
        at = pl.multiple_of(g * GROUP * (depth + 1), GROUP * (depth + 1))
        return jnp.concatenate(
            [y_ref[pl.ds(at + h * (depth + 1), depth), :] for h in range(GROUP)], axis=0
        )

    @pl.loop(0, groups // 4)
    def _(q):
        for k in range(4):
            own_ref[q * 4 + k] = bins_of(q * 4 + k).T[:ch].astype(jnp.bfloat16)

    for r in (1, 2):
        flag, body = sends[r - 1]
        flag.wait()
        body.wait()
        other = far_flag[r - 1][0:1, :]
        ref = own_x if r == 1 else far_x.at[r - 2]
        row = ref[ch - 1 : ch].astype(jnp.float32)
        prior = jnp.where(lax.rem(me + r, n) == 0, zero_row, row)
        whiten_block(far_x[r - 1], prior, other, table_ref, diff_ref, rows_ref, y_ref)

        @pl.loop(0, groups // 4)
        def _(q):
            for k in range(4):
                g = q * 4 + k
                at = pl.multiple_of(g * wide, wide)
                far_ref[r - 1, pl.ds(at, wide)] = bins_of(g).astype(jnp.bfloat16)

        count = jnp.sum(flags * other, axis=1, keepdims=True) * (1.0 / ch)
        scale_ref[r - 1] = jnp.broadcast_to(1.0 / jnp.maximum(count, 1.0), scale_ref.shape[1:])


def cross_kernel(own_ref, far_ref, scale_ref, inverse_ref, out_ref, t_ref):
    groups, ch, wide = own_ref.shape
    depth = wide // GROUP
    bins = groups * GROUP
    stage = pl.program_id(1)

    @pl.when(stage == 0)
    def _():
        scale = scale_ref[0][0:1, :]
        scale2 = jnp.concatenate([scale, scale], axis=1)

        def cross_group(g, carry):
            lhs = own_ref[g]
            far = far_ref[0, pl.ds(pl.multiple_of(g * wide, wide), wide), :]
            zero = jnp.zeros((depth, 2 * ch), jnp.bfloat16)
            for q in range(GROUP // 2):
                columns = []
                for h in (2 * q, 2 * q + 1):
                    parts = [zero] * GROUP
                    parts[h] = far[h * depth : (h + 1) * depth]
                    columns.append(jnp.concatenate(parts, axis=0))
                rhs = jnp.concatenate(columns, axis=1)
                cross = jnp.dot(lhs, rhs, preferred_element_type=jnp.float32) * scale2
                for s in (0, 1):
                    at = pl.multiple_of(g * GROUP * (ch + 1), GROUP * (ch + 1))
                    at = at + (2 * q + s) * (ch + 1)
                    t_ref[pl.ds(at, ch), :] = cross[:, s * 2 * ch : (s + 1) * 2 * ch]
            return carry

        lax.fori_loop(0, groups, cross_group, 0, unroll=UNROLL)

    @pl.when(stage > 0)
    def _():
        rows = out_ref.shape[1]
        per = 8

        @pl.loop(0, rows // per)
        def _(p):
            stacked = []
            for k in range(per):
                i = (stage - 1) * rows + p * per + k
                block = t_ref[pl.ds(i, bins, stride=ch + 1), :].astype(jnp.bfloat16).T
                stacked.append(jnp.concatenate([block[:ch], block[ch:]], axis=1))
            lhs = jnp.concatenate(stacked, axis=0)
            result = jnp.dot(lhs, inverse_ref[...], preferred_element_type=jnp.float32)
            result = result.astype(jnp.bfloat16).reshape(per, ch, result.shape[1])
            out_ref[0, pl.ds(p * per, per)] = result


def shards(traces, valid):
    n = lax.axis_size("blk")
    ch, windows, samples = traces.shape
    bins = samples // 2
    depth = 2 * windows
    vmem = pl.BlockSpec(memory_space=pltpu.VMEM)
    flags = jnp.broadcast_to(
        jnp.repeat(valid.astype(jnp.float32), ch, axis=1), (8, ch * windows)
    )
    own, far, scale = pl.pallas_call(
        functools.partial(gather_kernel, n),
        out_shape=(
            jax.ShapeDtypeStruct((bins // GROUP, ch, GROUP * depth), jnp.bfloat16),
            jax.ShapeDtypeStruct((ROUNDS, bins * depth, 2 * ch), jnp.bfloat16),
            jax.ShapeDtypeStruct((ROUNDS, 8, 2 * ch), jnp.float32),
        ),
        in_specs=[pl.BlockSpec(memory_space=pl.ANY), vmem, vmem],
        out_specs=(vmem, vmem, vmem),
        scratch_shapes=[
            pltpu.VMEM((ch, windows, samples), jnp.bfloat16),
            pltpu.VMEM((ROUNDS, ch, windows, samples), jnp.bfloat16),
            pltpu.VMEM((1, windows, samples), jnp.bfloat16),
            pltpu.VMEM((ROUNDS, 8, ch * windows), jnp.float32),
            pltpu.VMEM((samples // 128, ch * (windows + 1), 128), jnp.float32),
            pltpu.VMEM((ch * windows, samples), jnp.bfloat16),
            pltpu.VMEM((bins * (depth + 1), 2 * ch), jnp.float32),
            pltpu.SemaphoreType.DMA,
            pltpu.SemaphoreType.DMA((5,)),
            pltpu.SemaphoreType.DMA((5,)),
        ],
        compiler_params=pltpu.CompilerParams(
            collective_id=0, has_side_effects=True, vmem_limit_bytes=48 << 20
        ),
        name="gather_whiten",
    )(traces, flags, forward_table(samples))
    stages = 1 + ch // ROWS
    result = pl.pallas_call(
        cross_kernel,
        grid=(ROUNDS, stages),
        out_shape=jax.ShapeDtypeStruct((ROUNDS, ch, ch, LAGS), jnp.bfloat16),
        in_specs=[
            pl.BlockSpec(own.shape, lambda r, s: (0, 0, 0)),
            pl.BlockSpec((1,) + far.shape[1:], lambda r, s: (r, 0, 0)),
            pl.BlockSpec((1,) + scale.shape[1:], lambda r, s: (r, 0, 0)),
            pl.BlockSpec((2 * bins, LAGS), lambda r, s: (0, 0)),
        ],
        out_specs=pl.BlockSpec(
            (1, ROWS, ch, LAGS), lambda r, s: (r, jnp.maximum(s - 1, 0), 0, 0)
        ),
        scratch_shapes=[pltpu.VMEM((bins * (ch + 1), 2 * ch), jnp.float32)],
        compiler_params=pltpu.CompilerParams(
            dimension_semantics=("arbitrary", "arbitrary"), vmem_limit_bytes=48 << 20
        ),
        name="cross_inverse",
    )(own, far, scale, inverse_table(samples))
    return result[:, None]


def solution(mesh):
    return jax.shard_map(
        shards,
        mesh=mesh,
        in_specs=(P(("days", "blk"), None, None), P(("days", "blk"), None)),
        out_specs=P(None, ("days", "blk"), None, None, None),
        check_vma=False,
    )
```

```python
import functools
import math

import jax
import jax.numpy as jnp
import numpy as np
from jax import lax
from jax.experimental import pallas as pl
from jax.experimental.pallas import tpu as pltpu
from jax.sharding import PartitionSpec as P

LAGS = 512
BAND = 64
ROUNDS = 2
epsilon = 1e-05
GROUP = 8
ROWS = 8
UNROLL = 4


def forward_table(samples):
    bins = samples // 2
    phase = (np.arange(bins)[:, None] * np.arange(samples)[None, :] % samples) * (
        2.0 * math.pi / samples
    )
    cos = (np.cos(phase) / math.sqrt(samples)).reshape(bins // BAND, 1, BAND, samples)
    sin = (-np.sin(phase) / math.sqrt(samples)).reshape(bins // BAND, 1, BAND, samples)
    table = np.concatenate([cos, sin], axis=1).reshape(2 * bins, samples)
    return jnp.asarray(table.astype(np.float32), dtype=jnp.bfloat16)


def inverse_table(samples):
    bins = samples // 2
    shifts = np.arange(LAGS) - LAGS // 2
    phase = (np.arange(bins)[:, None] * shifts[None, :] % samples) * (2.0 * math.pi / samples)
    weight = np.where(np.arange(bins) == 0, 1.0, 2.0)[:, None] / math.sqrt(bins)
    table = np.concatenate([weight * np.cos(phase), -weight * np.sin(phase)], axis=0)
    return jnp.asarray(table.astype(np.float32), dtype=jnp.bfloat16)


def whiten_block(x, prior, flags, table_ref, diff_ref, rows_ref, y_ref):
    ch, windows, samples = x.shape
    bins = samples // 2
    wide = x.astype(jnp.float32)
    before = jnp.concatenate([prior.astype(jnp.float32), wide[:-1]], axis=0)
    diff = wide - before
    lanes = diff_ref.shape[2]
    pitch = windows + 1
    for q in range(samples // lanes):
        for c in range(ch):
            diff_ref[q, c * pitch : c * pitch + windows] = diff[c, :, q * lanes : (q + 1) * lanes]
        for w in range(windows):
            rows_ref[w * ch : (w + 1) * ch, q * lanes : (q + 1) * lanes] = diff_ref[
                q, pl.ds(w, ch, stride=pitch), :
            ].astype(jnp.bfloat16)
    bands = 2
    height = bands * 2 * BAND
    pitch = 2 * windows + 1

    @pl.loop(0, 2 * bins // height)
    def _(step):
        at = pl.multiple_of(step * height, height)
        product = lax.dot_general(
            table_ref[pl.ds(at, height), :],
            rows_ref[...],
            (((1,), (1,)), ((), ())),
            preferred_element_type=jnp.float32,
        )
        for k in range(bands):
            real = product[k * 2 * BAND : k * 2 * BAND + BAND]
            imag = product[k * 2 * BAND + BAND : (k + 1) * 2 * BAND]
            level = jnp.sum(real * real + imag * imag, axis=0, keepdims=True) * (1.0 / BAND)
            factor = lax.rsqrt(level + epsilon) * flags
            real = real * factor
            imag = imag * factor
            first = pl.multiple_of((step * bands + k) * BAND * pitch, BAND * pitch)
            for w in range(windows):
                re = real[:, w * ch : (w + 1) * ch]
                im = imag[:, w * ch : (w + 1) * ch]
                y_ref[pl.ds(first + w, BAND, stride=pitch), :] = jnp.concatenate([re, im], axis=1)
                y_ref[pl.ds(first + windows + w, BAND, stride=pitch), :] = jnp.concatenate(
                    [im, -re], axis=1
                )


def flag_lanes(flag_ref, ch):
    return jnp.concatenate(
        [jnp.full((1, ch), flag_ref[0, w], jnp.float32) for w in range(flag_ref.shape[1])], axis=1
    )


def prior_row(prior_ref, first):
    row = prior_ref[...].astype(jnp.float32)
    return jnp.where(first, jnp.zeros_like(row), row)


def bins_of(y_ref, g, depth):
    at = pl.multiple_of(g * GROUP * (depth + 1), GROUP * (depth + 1))
    return jnp.concatenate(
        [y_ref[pl.ds(at + h * (depth + 1), depth), :] for h in range(GROUP)], axis=0
    )


def own_kernel(x_ref, prior_ref, flag_ref, table_ref, own_ref, diff_ref, rows_ref, y_ref):
    ch, windows, _ = x_ref.shape
    first = lax.axis_index("blk") == 0
    whiten_block(
        x_ref[...],
        prior_row(prior_ref, first),
        flag_lanes(flag_ref, ch),
        table_ref,
        diff_ref,
        rows_ref,
        y_ref,
    )

    @pl.loop(0, own_ref.shape[0] // 4)
    def _(q):
        for k in range(4):
            block = bins_of(y_ref, q * 4 + k, 2 * windows)
            own_ref[q * 4 + k] = block.T[:ch].astype(jnp.bfloat16)


def round_kernel(
    distance,
    n,
    flag_ref,
    far_flag_ref,
    x_ref,
    prior_ref,
    own_ref,
    table_ref,
    inverse_ref,
    *rest,
):
    out_ref, diff_ref, rows_ref, y_ref, t_ref = rest[-5:]
    groups, ch, wide = own_ref.shape
    windows = flag_ref.shape[1]
    depth = wide // GROUP
    bins = groups * GROUP
    stage = pl.program_id(0)

    @pl.when(stage == 0)
    def _():
        first = lax.rem(lax.axis_index("blk") + distance, n) == 0
        whiten_block(
            x_ref[...],
            prior_row(prior_ref, first),
            flag_lanes(far_flag_ref, ch),
            table_ref,
            diff_ref,
            rows_ref,
            y_ref,
        )
        count = sum(flag_ref[0, w] * far_flag_ref[0, w] for w in range(windows))
        scale = 1.0 / jnp.maximum(jnp.full((1, 4 * ch), count, jnp.float32), 1.0)

        def cross_group(g, carry):
            lhs = own_ref[g]
            far = bins_of(y_ref, g, depth).astype(jnp.bfloat16)
            zero = jnp.zeros((depth, 2 * ch), jnp.bfloat16)
            for q in range(GROUP // 2):
                columns = []
                for h in (2 * q, 2 * q + 1):
                    parts = [zero] * GROUP
                    parts[h] = far[h * depth : (h + 1) * depth]
                    columns.append(jnp.concatenate(parts, axis=0))
                rhs = jnp.concatenate(columns, axis=1)
                cross = jnp.dot(lhs, rhs, preferred_element_type=jnp.float32) * scale
                for s in (0, 1):
                    at = pl.multiple_of(g * GROUP * (ch + 1), GROUP * (ch + 1))
                    at = at + (2 * q + s) * (ch + 1)
                    t_ref[pl.ds(at, ch), :] = cross[:, s * 2 * ch : (s + 1) * 2 * ch]
            return carry

        lax.fori_loop(0, groups, cross_group, 0, unroll=UNROLL)

    @pl.when(stage > 0)
    def _():
        rows = out_ref.shape[1]
        stacked = []
        for k in range(rows):
            i = (stage - 1) * rows + k
            block = t_ref[pl.ds(i, bins, stride=ch + 1), :].astype(jnp.bfloat16).T
            stacked.append(jnp.concatenate([block[:ch], block[ch:]], axis=1))
        lhs = jnp.concatenate(stacked, axis=0)
        result = jnp.dot(lhs, inverse_ref[...], preferred_element_type=jnp.float32)
        out_ref[0] = result.astype(jnp.bfloat16).reshape(rows, ch, result.shape[1])


def shards(traces, valid):
    n = lax.axis_size("blk")
    ch, windows, samples = traces.shape
    bins = samples // 2
    depth = 2 * windows

    def behind(value, distance):
        return lax.ppermute(value, "blk", [((i + distance) % n, i) for i in range(n)])

    before = behind(traces[ch - 1 :], -1)
    blocks = [traces] + [behind(traces, r) for r in range(1, ROUNDS + 1)]
    wire = valid.astype(jnp.bfloat16)
    flags = [wire] + [behind(wire, r) for r in range(1, ROUNDS + 1)]
    flags = [f.astype(jnp.float32) for f in flags]
    table = forward_table(samples)
    inverse = inverse_table(samples)

    smem = pl.BlockSpec(memory_space=pltpu.SMEM)
    vmem = pl.BlockSpec(memory_space=pltpu.VMEM)
    scratch = [
        pltpu.VMEM((samples // 128, ch * (windows + 1), 128), jnp.float32),
        pltpu.VMEM((ch * windows, samples), jnp.bfloat16),
        pltpu.VMEM((bins * (depth + 1), 2 * ch), jnp.float32),
    ]
    dft_flops = 2 * ch * windows * samples * samples
    own = pl.pallas_call(
        own_kernel,
        out_shape=jax.ShapeDtypeStruct((bins // GROUP, ch, GROUP * depth), jnp.bfloat16),
        in_specs=[vmem, vmem, smem, vmem],
        out_specs=vmem,
        scratch_shapes=scratch,
        compiler_params=pltpu.CompilerParams(vmem_limit_bytes=48 << 20),
        cost_estimate=pl.CostEstimate(
            flops=4 * dft_flops, bytes_accessed=8 << 20, transcendentals=0
        ),
        name="whiten_own",
    )(traces, before, flags[0], table)

    stages = 1 + ch // ROWS
    once = pl.Buffered(1)
    result = None
    for r in range(1, ROUNDS + 1):
        operands = [flags[0], flags[r], blocks[r], blocks[r - 1], own, table, inverse]
        in_specs = [
            smem,
            smem,
            pl.BlockSpec((ch, windows, samples), lambda s: (0, 0, 0), pipeline_mode=once),
            pl.BlockSpec((1, windows, samples), lambda s: (ch - 1, 0, 0), pipeline_mode=once),
            pl.BlockSpec(own.shape, lambda s: (0, 0, 0), pipeline_mode=once),
            pl.BlockSpec(table.shape, lambda s: (0, 0), pipeline_mode=once),
            pl.BlockSpec(inverse.shape, lambda s: (0, 0), pipeline_mode=once),
        ]
        alias = {}
        if result is not None:
            alias = {len(operands): 0}
            operands.append(result)
            in_specs.append(pl.BlockSpec(memory_space=pl.ANY))
        result = pl.pallas_call(
            functools.partial(round_kernel, r, n),
            grid=(stages,),
            out_shape=jax.ShapeDtypeStruct((ROUNDS, ch, ch, LAGS), jnp.bfloat16),
            in_specs=in_specs,
            out_specs=pl.BlockSpec(
                (1, ROWS, ch, LAGS), lambda s, r=r: (r - 1, jnp.maximum(s - 1, 0), 0, 0)
            ),
            scratch_shapes=scratch + [pltpu.VMEM((bins * (ch + 1), 2 * ch), jnp.float32)],
            input_output_aliases=alias,
            compiler_params=pltpu.CompilerParams(vmem_limit_bytes=48 << 20),
            cost_estimate=pl.CostEstimate(
                flops=16 * dft_flops, bytes_accessed=16 << 20, transcendentals=0
            ),
            name=f"round_{r}",
        )(*operands)
    return result[:, None]


def solution(mesh):
    return jax.shard_map(
        shards,
        mesh=mesh,
        in_specs=(P(("days", "blk"), None, None), P(("days", "blk"), None)),
        out_specs=P(None, ("days", "blk"), None, None, None),
        check_vma=False,
    )
```

```python
import functools
import math

import jax
import jax.numpy as jnp
import numpy as np
from jax import lax
from jax.experimental import pallas as pl
from jax.experimental.pallas import tpu as pltpu
from jax.sharding import PartitionSpec as P

LAGS = 512
BAND = 64
ROUNDS = 2
epsilon = 1e-05
GROUP = 8
ROWS = 8
UNROLL = 16
VMEM_BYTES = 48 << 20


def forward_table(samples):
    bins = samples // 2
    phase = (np.arange(bins)[:, None] * np.arange(samples)[None, :] % samples) * (
        2.0 * math.pi / samples
    )
    cos = (np.cos(phase) / math.sqrt(samples)).reshape(bins // BAND, 1, BAND, samples)
    sin = (-np.sin(phase) / math.sqrt(samples)).reshape(bins // BAND, 1, BAND, samples)
    table = np.concatenate([cos, sin], axis=1).reshape(2 * bins, samples)
    return jnp.asarray(table.astype(np.float32), dtype=jnp.bfloat16)


def inverse_table(samples):
    bins = samples // 2
    shifts = np.arange(LAGS) - LAGS // 2
    phase = (np.arange(bins)[:, None] * shifts[None, :] % samples) * (2.0 * math.pi / samples)
    weight = np.where(np.arange(bins) == 0, 1.0, 2.0)[:, None] / math.sqrt(bins)
    table = np.concatenate([weight * np.cos(phase), -weight * np.sin(phase)], axis=0)
    return jnp.asarray(table.astype(np.float32), dtype=jnp.bfloat16)


def whiten_block(x, prior, flags, table_ref, diff_ref, rows_ref, y_ref, ready=None):
    ch, windows, samples = x.shape
    bins = samples // 2
    wide = x.astype(jnp.float32)
    before = jnp.concatenate([prior.astype(jnp.float32), wide[:-1]], axis=0)
    diff = wide - before
    lanes = diff_ref.shape[2]
    pitch = windows + 1
    for q in range(samples // lanes):
        for c in range(ch):
            diff_ref[q, c * pitch : c * pitch + windows] = diff[c, :, q * lanes : (q + 1) * lanes]
        for w in range(windows):
            rows_ref[w * ch : (w + 1) * ch, q * lanes : (q + 1) * lanes] = diff_ref[
                q, pl.ds(w, ch, stride=pitch), :
            ].astype(jnp.bfloat16)
    if ready is not None:
        ready()
    bands = 2
    height = bands * 2 * BAND
    pitch = 2 * windows + 1

    @pl.loop(0, 2 * bins // height)
    def _(step):
        at = pl.multiple_of(step * height, height)
        product = lax.dot_general(
            table_ref[pl.ds(at, height), :],
            rows_ref[...],
            (((1,), (1,)), ((), ())),
            preferred_element_type=jnp.float32,
        )
        for k in range(bands):
            real = product[k * 2 * BAND : k * 2 * BAND + BAND]
            imag = product[k * 2 * BAND + BAND : (k + 1) * 2 * BAND]
            level = jnp.sum(real * real + imag * imag, axis=0, keepdims=True) * (1.0 / BAND)
            factor = lax.rsqrt(level + epsilon) * flags
            real = real * factor
            imag = imag * factor
            first = pl.multiple_of((step * bands + k) * BAND * pitch, BAND * pitch)
            for w in range(windows):
                re = real[:, w * ch : (w + 1) * ch]
                im = imag[:, w * ch : (w + 1) * ch]
                y_ref[pl.ds(first + w, BAND, stride=pitch), :] = jnp.concatenate([re, im], axis=1)
                y_ref[pl.ds(first + windows + w, BAND, stride=pitch), :] = jnp.concatenate(
                    [im, -re], axis=1
                )


def flag_lanes(flag_ref, ch):
    row = flag_ref[0].astype(jnp.float32)
    return jnp.concatenate([row[w : w + 1, :ch] for w in range(row.shape[0])], axis=1)


def prior_row(prior_ref, first):
    row = prior_ref[...].astype(jnp.float32)
    return jnp.where(first, jnp.zeros_like(row), row)


def bins_of(y_ref, g, depth):
    at = pl.multiple_of(g * GROUP * (depth + 1), GROUP * (depth + 1))
    return jnp.concatenate(
        [y_ref[pl.ds(at + h * (depth + 1), depth), :] for h in range(GROUP)], axis=0
    )


def own_kernel(
    x_ref, prior_ref, flag_ref, table_hbm, own_ref, table_ref, sem, diff_ref, rows_ref, y_ref
):
    fetch = pltpu.make_async_copy(table_hbm, table_ref, sem)
    fetch.start()
    ch, windows, _ = x_ref.shape
    first = lax.axis_index("blk") == 0
    whiten_block(
        x_ref[...],
        prior_row(prior_ref, first),
        flag_lanes(flag_ref, ch),
        table_ref,
        diff_ref,
        rows_ref,
        y_ref,
        fetch.wait,
    )

    @pl.loop(0, own_ref.shape[0] // 4)
    def _(q):
        for k in range(4):
            block = bins_of(y_ref, q * 4 + k, 2 * windows)
            own_ref[q * 4 + k] = block.T[:ch].astype(jnp.bfloat16)


def round_kernel(
    distance,
    n,
    flag_ref,
    far_flag_ref,
    x_ref,
    prior_ref,
    own_ref,
    table_ref,
    inverse_ref,
    *rest,
):
    out_ref, diff_ref, rows_ref, y_ref, t_ref = rest[-5:]
    groups, ch, wide = own_ref.shape
    windows = flag_ref.shape[1]
    depth = wide // GROUP
    bins = groups * GROUP
    stage = pl.program_id(0)

    @pl.when(stage == 0)
    def _():
        first = lax.rem(lax.axis_index("blk") + distance, n) == 0
        whiten_block(
            x_ref[...],
            prior_row(prior_ref, first),
            flag_lanes(far_flag_ref, ch),
            table_ref,
            diff_ref,
            rows_ref,
            y_ref,
        )
        shared = flag_ref[0].astype(jnp.float32) * far_flag_ref[0].astype(jnp.float32)
        count = jnp.sum(shared[:, : 4 * ch], axis=0, keepdims=True)
        scale = 1.0 / jnp.maximum(count, 1.0)

        def cross_group(g, carry):
            lhs = own_ref[g]
            far = bins_of(y_ref, g, depth).astype(jnp.bfloat16)
            zero = jnp.zeros((depth, 2 * ch), jnp.bfloat16)
            for q in range(GROUP // 2):
                columns = []
                for h in (2 * q, 2 * q + 1):
                    parts = [zero] * GROUP
                    parts[h] = far[h * depth : (h + 1) * depth]
                    columns.append(jnp.concatenate(parts, axis=0))
                rhs = jnp.concatenate(columns, axis=1)
                cross = jnp.dot(lhs, rhs, preferred_element_type=jnp.float32) * scale
                for s in (0, 1):
                    at = pl.multiple_of(g * GROUP * (ch + 1), GROUP * (ch + 1))
                    at = at + (2 * q + s) * (ch + 1)
                    t_ref[pl.ds(at, ch), :] = cross[:, s * 2 * ch : (s + 1) * 2 * ch]
            return carry

        lax.fori_loop(0, groups, cross_group, 0, unroll=UNROLL)

    @pl.when(stage > 0)
    def _():
        rows = out_ref.shape[1]
        stacked = []
        for k in range(rows):
            i = (stage - 1) * rows + k
            block = t_ref[pl.ds(i, bins, stride=ch + 1), :].astype(jnp.bfloat16).T
            stacked.append(jnp.concatenate([block[:ch], block[ch:]], axis=1))
        lhs = jnp.concatenate(stacked, axis=0)
        result = jnp.dot(lhs, inverse_ref[...], preferred_element_type=jnp.float32)
        out_ref[0] = result.astype(jnp.bfloat16).reshape(rows, ch, result.shape[1])


def shards(traces, valid):
    n = lax.axis_size("blk")
    ch, windows, samples = traces.shape
    bins = samples // 2
    depth = 2 * windows

    def behind(value, distance):
        return lax.ppermute(value, "blk", [((i + distance) % n, i) for i in range(n)])

    before = behind(traces[ch - 1 :], -1)
    row = jnp.broadcast_to(valid.astype(jnp.bfloat16)[:, :, None], (1, windows, samples))
    tagged = jnp.concatenate([traces, row], axis=0)
    blocks = [tagged] + [behind(tagged, r) for r in range(1, ROUNDS + 1)]
    table = forward_table(samples)
    inverse = inverse_table(samples)

    once = pl.Buffered(1)

    def whole(shape):
        return pl.BlockSpec(shape, lambda s: (0,) * len(shape), pipeline_mode=once)

    def row_at(at):
        return pl.BlockSpec((1, windows, samples), lambda s: (at, 0, 0), pipeline_mode=once)

    block = whole((ch, windows, samples))
    scratch = [
        pltpu.VMEM((samples // 128, ch * (windows + 1), 128), jnp.float32),
        pltpu.VMEM((ch * windows, samples), jnp.bfloat16),
        pltpu.VMEM((bins * (depth + 1), 2 * ch), jnp.float32),
    ]
    dft_flops = 2 * ch * windows * samples * samples
    own = pl.pallas_call(
        own_kernel,
        out_shape=jax.ShapeDtypeStruct((bins // GROUP, ch, GROUP * depth), jnp.bfloat16),
        grid=(1,),
        in_specs=[block, row_at(0), row_at(ch), pl.BlockSpec(memory_space=pl.ANY)],
        out_specs=whole((bins // GROUP, ch, GROUP * depth)),
        scratch_shapes=[
            pltpu.VMEM((2 * bins, samples), jnp.bfloat16),
            pltpu.SemaphoreType.DMA,
        ]
        + scratch,
        compiler_params=pltpu.CompilerParams(vmem_limit_bytes=VMEM_BYTES),
        cost_estimate=pl.CostEstimate(
            flops=4 * dft_flops, bytes_accessed=8 << 20, transcendentals=0
        ),
        name="whiten_own",
    )(traces, before, tagged, table)

    stages = 1 + ch // ROWS
    result = None
    for r in range(1, ROUNDS + 1):
        operands = [tagged, blocks[r], blocks[r], blocks[r - 1], own, table, inverse]
        in_specs = [
            row_at(ch),
            row_at(ch),
            block,
            row_at(ch - 1),
            whole(own.shape),
            whole(table.shape),
            whole(inverse.shape),
        ]
        alias = {}
        if result is not None:
            alias = {len(operands): 0}
            operands.append(result)
            in_specs.append(pl.BlockSpec(memory_space=pl.ANY))
        result = pl.pallas_call(
            functools.partial(round_kernel, r, n),
            grid=(stages,),
            out_shape=jax.ShapeDtypeStruct((ROUNDS, ch, ch, LAGS), jnp.bfloat16),
            in_specs=in_specs,
            out_specs=pl.BlockSpec(
                (1, ROWS, ch, LAGS), lambda s, r=r: (r - 1, jnp.maximum(s - 1, 0), 0, 0)
            ),
            scratch_shapes=scratch + [pltpu.VMEM((bins * (ch + 1), 2 * ch), jnp.float32)],
            input_output_aliases=alias,
            compiler_params=pltpu.CompilerParams(vmem_limit_bytes=VMEM_BYTES),
            cost_estimate=pl.CostEstimate(
                flops=16 * dft_flops, bytes_accessed=16 << 20, transcendentals=0
            ),
            name=f"round_{r}",
        )(*operands)
    return result[:, None]


def solution(mesh):
    return jax.shard_map(
        shards,
        mesh=mesh,
        in_specs=(P(("days", "blk"), None, None), P(("days", "blk"), None)),
        out_specs=P(None, ("days", "blk"), None, None, None),
        check_vma=False,
    )
```

```python
import functools
import math

import jax
import jax.numpy as jnp
import numpy as np
from jax import lax
from jax.experimental import pallas as pl
from jax.experimental.pallas import tpu as pltpu
from jax.sharding import PartitionSpec as P

LAGS = 512
BAND = 64
ROUNDS = 2
epsilon = 1e-05
GROUP = 8
ROWS = 8
UNROLL = 16
VMEM_BYTES = 48 << 20


def forward_table(samples):
    bins = samples // 2
    phase = (np.arange(bins)[:, None] * np.arange(samples)[None, :] % samples) * (
        2.0 * math.pi / samples
    )
    cos = (np.cos(phase) / math.sqrt(samples)).reshape(bins // BAND, 1, BAND, samples)
    sin = (-np.sin(phase) / math.sqrt(samples)).reshape(bins // BAND, 1, BAND, samples)
    table = np.concatenate([cos, sin], axis=1).reshape(2 * bins, samples)
    return jnp.asarray(table.astype(np.float32), dtype=jnp.bfloat16)


def inverse_table(samples):
    bins = samples // 2
    shifts = np.arange(LAGS) - LAGS // 2
    phase = (np.arange(bins)[:, None] * shifts[None, :] % samples) * (2.0 * math.pi / samples)
    weight = np.where(np.arange(bins) == 0, 1.0, 2.0)[:, None] / math.sqrt(bins)
    table = np.concatenate([weight * np.cos(phase), -weight * np.sin(phase)], axis=0)
    return jnp.asarray(table.astype(np.float32), dtype=jnp.bfloat16)


def whiten_block(x, prior, flags, table_ref, diff_ref, rows_ref, y_ref, ready=None):
    ch, windows, samples = x.shape
    bins = samples // 2
    wide = x.astype(jnp.float32)
    before = jnp.concatenate([prior.astype(jnp.float32), wide[:-1]], axis=0)
    diff = wide - before
    lanes = diff_ref.shape[2]
    pitch = windows + 1
    for q in range(samples // lanes):
        for c in range(ch):
            diff_ref[q, c * pitch : c * pitch + windows] = diff[c, :, q * lanes : (q + 1) * lanes]
        for w in range(windows):
            rows_ref[w * ch : (w + 1) * ch, q * lanes : (q + 1) * lanes] = diff_ref[
                q, pl.ds(w, ch, stride=pitch), :
            ].astype(jnp.bfloat16)
    if ready is not None:
        ready()
    bands = 2
    height = bands * 2 * BAND
    pitch = 2 * windows + 1

    @pl.loop(0, 2 * bins // height)
    def _(step):
        at = pl.multiple_of(step * height, height)
        product = lax.dot_general(
            table_ref[pl.ds(at, height), :],
            rows_ref[...],
            (((1,), (1,)), ((), ())),
            preferred_element_type=jnp.float32,
        )
        for k in range(bands):
            real = product[k * 2 * BAND : k * 2 * BAND + BAND]
            imag = product[k * 2 * BAND + BAND : (k + 1) * 2 * BAND]
            level = jnp.sum(real * real + imag * imag, axis=0, keepdims=True) * (1.0 / BAND)
            factor = lax.rsqrt(level + epsilon) * flags
            real = real * factor
            imag = imag * factor
            first = pl.multiple_of((step * bands + k) * BAND * pitch, BAND * pitch)
            for w in range(windows):
                re = real[:, w * ch : (w + 1) * ch]
                im = imag[:, w * ch : (w + 1) * ch]
                y_ref[pl.ds(first + w, BAND, stride=pitch), :] = jnp.concatenate([re, im], axis=1)
                y_ref[pl.ds(first + windows + w, BAND, stride=pitch), :] = jnp.concatenate(
                    [im, -re], axis=1
                )


def flag_lanes(flag_ref, ch):
    row = flag_ref[0].astype(jnp.float32)
    return jnp.concatenate([row[w : w + 1, :ch] for w in range(row.shape[0])], axis=1)


def prior_row(prior_ref, first):
    row = prior_ref[...].astype(jnp.float32)
    return jnp.where(first, jnp.zeros_like(row), row)


def bins_of(y_ref, g, depth):
    at = pl.multiple_of(g * GROUP * (depth + 1), GROUP * (depth + 1))
    return jnp.concatenate(
        [y_ref[pl.ds(at + h * (depth + 1), depth), :] for h in range(GROUP)], axis=0
    )


def own_kernel(
    x_ref, prior_ref, flag_ref, table_hbm, own_ref, table_ref, sem, diff_ref, rows_ref, y_ref
):
    fetch = pltpu.make_async_copy(table_hbm, table_ref, sem)
    fetch.start()
    ch, windows, _ = x_ref.shape
    first = lax.axis_index("blk") == 0
    whiten_block(
        x_ref[...],
        prior_row(prior_ref, first),
        flag_lanes(flag_ref, ch),
        table_ref,
        diff_ref,
        rows_ref,
        y_ref,
        fetch.wait,
    )

    @pl.loop(0, own_ref.shape[0] // 4)
    def _(q):
        for k in range(4):
            block = bins_of(y_ref, q * 4 + k, 2 * windows)
            own_ref[q * 4 + k] = block.T[:ch].astype(jnp.bfloat16)


def round_kernel(
    distance,
    n,
    flag_ref,
    far_flag_ref,
    x_ref,
    prior_ref,
    own_ref,
    table_ref,
    inverse_ref,
    *rest,
):
    out_ref, diff_ref, rows_ref, y_ref, t_ref = rest[-5:]
    groups, ch, wide = own_ref.shape
    windows = flag_ref.shape[1]
    depth = wide // GROUP
    bins = groups * GROUP
    stage = pl.program_id(0)

    @pl.when(stage == 0)
    def _():
        first = lax.rem(lax.axis_index("blk") + distance, n) == 0
        whiten_block(
            x_ref[...],
            prior_row(prior_ref, first),
            flag_lanes(far_flag_ref, ch),
            table_ref,
            diff_ref,
            rows_ref,
            y_ref,
        )
        shared = flag_ref[0].astype(jnp.float32) * far_flag_ref[0].astype(jnp.float32)
        count = jnp.sum(shared[:, : 4 * ch], axis=0, keepdims=True)
        scale = 1.0 / jnp.maximum(count, 1.0)

        def cross_group(g, carry):
            lhs = own_ref[g]
            far = bins_of(y_ref, g, depth).astype(jnp.bfloat16)
            zero = jnp.zeros((depth, 2 * ch), jnp.bfloat16)
            for q in range(GROUP // 2):
                columns = []
                for h in (2 * q, 2 * q + 1):
                    parts = [zero] * GROUP
                    parts[h] = far[h * depth : (h + 1) * depth]
                    columns.append(jnp.concatenate(parts, axis=0))
                rhs = jnp.concatenate(columns, axis=1)
                cross = jnp.dot(lhs, rhs, preferred_element_type=jnp.float32) * scale
                for s in (0, 1):
                    at = pl.multiple_of(g * GROUP * (ch + 1), GROUP * (ch + 1))
                    at = at + (2 * q + s) * (ch + 1)
                    t_ref[pl.ds(at, ch), :] = cross[:, s * 2 * ch : (s + 1) * 2 * ch]
            return carry

        lax.fori_loop(0, groups, cross_group, 0, unroll=UNROLL)

    @pl.when(stage > 0)
    def _():
        rows = out_ref.shape[1]
        stacked = []
        for k in range(rows):
            i = (stage - 1) * rows + k
            block = t_ref[pl.ds(i, bins, stride=ch + 1), :].astype(jnp.bfloat16).T
            stacked.append(jnp.concatenate([block[:ch], block[ch:]], axis=1))
        lhs = jnp.concatenate(stacked, axis=0)
        result = jnp.dot(lhs, inverse_ref[...], preferred_element_type=jnp.float32)
        out_ref[0] = result.astype(jnp.bfloat16).reshape(rows, ch, result.shape[1])


def shards(traces, valid):
    n = lax.axis_size("blk")
    ch, windows, samples = traces.shape
    bins = samples // 2
    depth = 2 * windows

    def behind(value, distance):
        return lax.ppermute(value, "blk", [((i + distance) % n, i) for i in range(n)])

    before = behind(traces[ch - 1 :], -1)
    row = jnp.broadcast_to(valid.astype(jnp.bfloat16)[:, :, None], (1, windows, samples))
    tagged = jnp.concatenate([traces, row], axis=0)
    near = behind(tagged, 1)
    later, near = lax.optimization_barrier((tagged, near))
    if n % 2 == 0:
        relayed = lax.ppermute(near, "blk", [(i + 1, i) for i in range(0, n, 2)])
        direct = lax.ppermute(later, "blk", [((i + 2) % n, i) for i in range(1, n, 2)])
        second = jnp.where(lax.axis_index("blk") % 2 == 0, relayed, direct)
    else:
        second = behind(later, 2)
    blocks = [tagged, near, second]
    table = forward_table(samples)
    inverse = inverse_table(samples)

    once = pl.Buffered(1)

    def whole(shape):
        return pl.BlockSpec(shape, lambda s: (0,) * len(shape), pipeline_mode=once)

    def row_at(at):
        return pl.BlockSpec((1, windows, samples), lambda s: (at, 0, 0), pipeline_mode=once)

    block = whole((ch, windows, samples))
    scratch = [
        pltpu.VMEM((samples // 128, ch * (windows + 1), 128), jnp.float32),
        pltpu.VMEM((ch * windows, samples), jnp.bfloat16),
        pltpu.VMEM((bins * (depth + 1), 2 * ch), jnp.float32),
    ]
    dft_flops = 2 * ch * windows * samples * samples
    own = pl.pallas_call(
        own_kernel,
        out_shape=jax.ShapeDtypeStruct((bins // GROUP, ch, GROUP * depth), jnp.bfloat16),
        grid=(1,),
        in_specs=[block, row_at(0), row_at(ch), pl.BlockSpec(memory_space=pl.ANY)],
        out_specs=whole((bins // GROUP, ch, GROUP * depth)),
        scratch_shapes=[
            pltpu.VMEM((2 * bins, samples), jnp.bfloat16),
            pltpu.SemaphoreType.DMA,
        ]
        + scratch,
        compiler_params=pltpu.CompilerParams(vmem_limit_bytes=VMEM_BYTES),
        cost_estimate=pl.CostEstimate(
            flops=4 * dft_flops, bytes_accessed=8 << 20, transcendentals=0
        ),
        name="whiten_own",
    )(traces, before, tagged, table)

    stages = 1 + ch // ROWS
    result = None
    for r in range(1, ROUNDS + 1):
        operands = [tagged, blocks[r], blocks[r], blocks[r - 1], own, table, inverse]
        in_specs = [
            row_at(ch),
            row_at(ch),
            block,
            row_at(ch - 1),
            whole(own.shape),
            whole(table.shape),
            whole(inverse.shape),
        ]
        alias = {}
        if result is not None:
            alias = {len(operands): 0}
            operands.append(result)
            in_specs.append(pl.BlockSpec(memory_space=pl.ANY))
        result = pl.pallas_call(
            functools.partial(round_kernel, r, n),
            grid=(stages,),
            out_shape=jax.ShapeDtypeStruct((ROUNDS, ch, ch, LAGS), jnp.bfloat16),
            in_specs=in_specs,
            out_specs=pl.BlockSpec(
                (1, ROWS, ch, LAGS), lambda s, r=r: (r - 1, jnp.maximum(s - 1, 0), 0, 0)
            ),
            scratch_shapes=scratch + [pltpu.VMEM((bins * (ch + 1), 2 * ch), jnp.float32)],
            input_output_aliases=alias,
            compiler_params=pltpu.CompilerParams(vmem_limit_bytes=VMEM_BYTES),
            cost_estimate=pl.CostEstimate(
                flops=16 * dft_flops, bytes_accessed=16 << 20, transcendentals=0
            ),
            name=f"round_{r}",
        )(*operands)
    return result[:, None]


def solution(mesh):
    return jax.shard_map(
        shards,
        mesh=mesh,
        in_specs=(P(("days", "blk"), None, None), P(("days", "blk"), None)),
        out_specs=P(None, ("days", "blk"), None, None, None),
        check_vma=False,
    )
```
